32 devices in a mesh: gx: 4 (over y, x), gy: 8 (over z, core).
Axes of the slice: x: 2, y: 2, z: 4, core: 2. Of those that a mesh axis runs over, the one named last changes fastest.
Arguments:
- fields: bfloat16 [8, 64, 128, 192], P(None, 'gx', 'gy'), may hold values from -6 to 6
- gain_window: float32 [192], replicated, may hold values from 0.1 to 1.9
- mixer_fine: bfloat16 [192, 576], replicated, may hold values from -3 to 3
- output_fine: bfloat16 [192, 192], replicated, may hold values from -0.4375 to 0.4375
- gain_hidden: float32 [192], replicated, may hold values from 0.1 to 1.9
- expand: bfloat16 [192, 768], replicated, may hold values from -0.4375 to 0.4375
- contract: bfloat16 [768, 192], replicated, may hold values from -0.21875 to 0.21875
- gain_merge: float32 [768], replicated, may hold values from 0.1 to 1.9
- merge_weight: bfloat16 [768, 384], replicated, may hold values from -0.21875 to 0.21875
- gain_coarse: float32 [384], replicated, may hold values from 0.1 to 1.9
- mixer_coarse: bfloat16 [384, 1152], replicated, may hold values from -2.1 to 2.1
- output_coarse: bfloat16 [384, 384], replicated, may hold values from -0.3125 to 0.3125
Outputs:
- merged: bfloat16 [8, 32, 64, 384], P(None, 'gx', 'gy')
- coarse: bfloat16 [8, 32, 64, 384], P(None, 'gx', 'gy')
The draws below stay inside these ranges and needn't reach their ends.
All inputs are finite; a program needn't handle non-finite values.
Results may differ from the reference program's by a relative error of at most 0.019.
Values may be sent and summed in bfloat16 or wider, within the bound.
A program may use at most 128 MiB of HBM per device.

```python
import math
import jax
import jax.numpy as jnp
from jax import lax

BATCH = 8
WIN = 16
C2 = 192
C3 = 384
HID2 = 768
HEADS2 = 6
HEADS3 = 12
H2 = 64
W2 = 128
H3 = 32
W3 = 64


def normal_block(key, rows_count, columns):
    return jax.random.truncated_normal(key, -5.0, 5.0, (rows_count, columns), jnp.float32) / math.sqrt(rows_count)


def draw_fields(key, part):
    key_base = jax.random.fold_in(key, 0)
    values = jax.random.truncated_normal(key_base, -6.0, 6.0, (BATCH, H2, W2, C2), jnp.float32)
    return values.astype(jnp.bfloat16)


def draw_mixer_fine(key, part):
    key_base = jax.random.fold_in(key, 0)
    base = normal_block(key_base, C2, 3 * C2)
    values = base
    return jnp.clip(values, -3.0, 3.0).astype(jnp.bfloat16)


def draw_mixer_coarse(key, part):
    key_base = jax.random.fold_in(jax.random.fold_in(key, 7), 0)
    base = normal_block(key_base, C3, 3 * C3)
    values = base
    return jnp.clip(values, -2.1, 2.1).astype(jnp.bfloat16)


def scatter_about(rng, shape, scale, bound, kind=jnp.bfloat16):
    return jnp.clip(scale * jax.random.normal(rng, shape, jnp.float32), -bound, bound).astype(kind)


def setup_inputs(seed: int = 0) -> dict:
    key_of = jax.random.split(jax.random.key(seed), 13)
    return {
        "fields": draw_fields(jax.random.fold_in(key_of[12], 71), 0),
        "gain_window": jnp.clip(1.0 + 0.18 * jax.random.normal(key_of[1], (C2,), jnp.float32), 0.1, 1.9),
        "mixer_fine": draw_mixer_fine(jax.random.fold_in(key_of[12], 71), 0),
        "output_fine": scatter_about(key_of[3], (C2, C2), C2 ** -0.5, 0.4375),
        "gain_hidden": jnp.clip(1.0 + 0.18 * jax.random.normal(key_of[4], (C2,), jnp.float32), 0.1, 1.9),
        "expand": scatter_about(key_of[5], (C2, HID2), C2 ** -0.5, 0.4375),
        "contract": scatter_about(key_of[6], (HID2, C2), HID2 ** -0.5, 0.21875),
        "gain_merge": jnp.clip(1.0 + 0.18 * jax.random.normal(key_of[7], (4 * C2,), jnp.float32), 0.1, 1.9),
        "merge_weight": scatter_about(key_of[8], (4 * C2, C3), (4 * C2) ** -0.5, 0.21875),
        "gain_coarse": jnp.clip(1.0 + 0.18 * jax.random.normal(key_of[9], (C3,), jnp.float32), 0.1, 1.9),
        "mixer_coarse": draw_mixer_coarse(jax.random.fold_in(key_of[12], 71), 0),
        "output_coarse": scatter_about(key_of[11], (C3, C3), C3 ** -0.5, 0.3125),
    }


epsilon = 1e-05

def normalize(values, scaling):
    values = values.astype(jnp.float32)
    center = values - lax.optimization_barrier(jnp.mean(values, -1, keepdims=True))
    spread = lax.optimization_barrier(jnp.mean(center * center, -1, keepdims=True))
    return center * lax.rsqrt(spread + epsilon) * scaling.astype(jnp.float32)

def attend(query_rows, key_rows, value_rows, head_count):
    windows, length, channels = query_rows.shape
    head_size = channels // head_count
    split_query = query_rows.astype(jnp.float32).reshape(windows, length, head_count, head_size)
    split_keys = key_rows.astype(jnp.float32).reshape(windows, -1, head_count, head_size)
    split_values = value_rows.astype(jnp.float32).reshape(windows, -1, head_count, head_size)
    scores = jnp.einsum('nqhd,nkhd->nhqk', split_query, split_keys) / math.sqrt(head_size)
    highest = lax.optimization_barrier(jnp.max(scores, -1, keepdims=True))
    powers = jnp.exp(scores - highest)
    attention = (powers / lax.optimization_barrier(jnp.sum(powers, -1, keepdims=True))).astype(jnp.bfloat16)
    context = jnp.einsum('nhqk,nkhd->nqhd', attention.astype(jnp.float32), split_values)
    return context.reshape(windows, length, channels).astype(jnp.bfloat16)

def attention_layer(tokens, scaling, mixer, output_weight, head_count):
    channels = tokens.shape[-1]
    normed = normalize(tokens, scaling).astype(jnp.bfloat16)
    projected = jnp.dot(normed, mixer, preferred_element_type=jnp.float32).astype(jnp.bfloat16)
    context = attend(projected[..., :channels], projected[..., channels:2 * channels], projected[..., 2 * channels:], head_count)
    update = jnp.dot(context, output_weight, preferred_element_type=jnp.float32)
    return (tokens.astype(jnp.float32) + update).astype(jnp.bfloat16)

def feed_forward(tokens, scaling, expand, contract):
    normed = normalize(tokens, scaling).astype(jnp.bfloat16)
    hidden = jax.nn.gelu(jnp.dot(normed, expand, preferred_element_type=jnp.float32), approximate=False).astype(jnp.bfloat16)
    return (tokens.astype(jnp.float32) + jnp.dot(hidden, contract, preferred_element_type=jnp.float32)).astype(jnp.bfloat16)

def merge_patches(tokens, scaling, merge_weight):
    samples, height, breadth, channels = tokens.shape
    patches = tokens.reshape(samples, height // 2, 2, breadth // 2, 2, channels).transpose(0, 1, 3, 4, 2, 5)
    patches = patches.reshape(samples, height // 2, breadth // 2, 4 * channels)
    normed = normalize(patches, scaling).astype(jnp.bfloat16)
    return jnp.dot(normed, merge_weight, preferred_element_type=jnp.float32).astype(jnp.bfloat16)

def to_windows(tokens, window):
    samples, height, breadth, channels = tokens.shape
    blocks = tokens.reshape(samples, height // window, window, breadth // window, window, channels)
    return blocks.transpose(0, 1, 3, 2, 4, 5).reshape(samples * (height // window), breadth // window, window * window, channels)

def from_windows(blocks, samples, height, breadth, window):
    channels = blocks.shape[-1]
    tokens = blocks.reshape(samples, height // window, breadth // window, window, window, channels)
    return tokens.transpose(0, 1, 3, 2, 4, 5).reshape(samples, height, breadth, channels)

def reference(fields, gain_window, mixer_fine, output_fine, gain_hidden, expand, contract, gain_merge, merge_weight, gain_coarse, mixer_coarse, output_coarse):
    offset = WIN // 2
    rolled = jnp.roll(fields, (-offset, -offset), axis=(1, 2))

    def fine_block(blocks):
        attended = attention_layer(blocks, gain_window, mixer_fine, output_fine, HEADS2)
        return feed_forward(attended, gain_hidden, expand, contract)
    refined = lax.map(fine_block, to_windows(rolled, WIN))
    refined = jnp.roll(from_windows(refined, BATCH, H2, W2, WIN), (offset, offset), axis=(1, 2))
    merged = lax.map(lambda sample: merge_patches(sample[None], gain_merge, merge_weight)[0], refined)

    def coarse_block(blocks):
        return attention_layer(blocks, gain_coarse, mixer_coarse, output_coarse, HEADS3)
    coarse = from_windows(lax.map(coarse_block, to_windows(merged, WIN)), BATCH, H3, W3, WIN)
    return (merged, coarse)
```

```python
import functools
import math

import jax
import jax.numpy as jnp
from jax import lax
from jax.experimental import pallas as pl
from jax.experimental.pallas import tpu as pltpu
from jax.sharding import PartitionSpec as P

HEAD = 32
LANES = 128
EPSILON = 1e-05
F32 = jnp.float32
BF16 = jnp.bfloat16
MESH = pl.DeviceIdType.MESH


def dot(a, b):
    return jnp.dot(a, b, preferred_element_type=F32)


def dot_nt(a, b):
    return lax.dot_general(a, b, (((1,), (1,)), ((), ())), preferred_element_type=F32)


def normalize(values, gain):
    center = values - jnp.mean(values, -1, keepdims=True)
    spread = jnp.mean(center * center, -1, keepdims=True)
    return (center * lax.rsqrt(spread + EPSILON) * gain).astype(BF16)


def gelu(x):
    return 0.5 * x * (1.0 + lax.erf(x * (1.0 / math.sqrt(2.0))))


def attention(queries, keys, values):
    channels = queries.shape[-1]
    factor = math.log2(math.e) / math.sqrt(HEAD)
    groups = []
    for low in range(0, channels, LANES):
        width = min(LANES, channels - low)
        q, k, v = (t[:, low : low + width] for t in (queries, keys, values))
        owner = lax.broadcasted_iota(jnp.int32, (1, width), 1) // HEAD
        context = None
        for head in range(width // HEAD):
            mine = owner == head
            scores = dot_nt(q * mine.astype(F32).astype(BF16), k)
            highest = jnp.max(scores, -1, keepdims=True)
            powers = jnp.exp2((scores - highest) * factor)
            total = jnp.sum(powers, -1, keepdims=True)
            part = dot(powers.astype(BF16), v) * (1.0 / total)
            context = part if context is None else jnp.where(mine, part, context)
        groups.append(context.astype(BF16))
    return groups


def project(groups, weight_ref):
    total = None
    for index, group in enumerate(groups):
        part = dot(group, weight_ref[index * LANES : index * LANES + group.shape[-1], :])
        total = part if total is None else total + part
    return total


def kernel(
    nx, ny,
    fields, *refs
):
    count = (len(refs) - 16) // 2
    weights_hbm, (mhome, coarse_out) = refs[:count], refs[count : count + 2]
    weights = refs[count + 2 : 2 * count + 2]
    (
        gain_window, mixer_fine, output_fine, gain_hidden, expand, contract,
        gain_merge, merge_weight, gain_coarse, mixer_coarse, output_coarse,
    ) = weights
    (
    fbuf, mbuf, cbuf, obuf, wsplit, perm_fine,
    f_send, f_recv, m_send, m_recv, c_send, c_recv, o_send, o_recv,
    w_recv,
    ) = refs[2 * count + 2 :]
    sets, _, _, half, _, channels = fbuf.shape
    side = 2 * half
    tokens = side * side
    quarter = half // 2
    piece = quarter * quarter
    patch = 4 * piece
    wide = mhome.shape[-1]
    x = lax.axis_index("gx")
    y = lax.axis_index("gy")
    px, py = x % 2, y % 2
    me = px * 2 + py

    def at(dx, dy):
        return (lax.rem(x + dx + nx, nx), lax.rem(y + dy + ny, ny))

    outx, outy = 2 * (2 * px - 1), 2 * (2 * py - 1)
    reach = [(dx, dy) for dx in (-1, 0, 1) for dy in (-1, 0, 1) if (dx, dy) != (0, 0)]
    for sign in (-1, 1):
        reach += [(sign * outx, 0), (0, sign * outy), (sign * outx, sign * outy)]
    barrier = pltpu.get_barrier_semaphore()
    for dx, dy in reach:
        pl.semaphore_signal(barrier, inc=1, device_id=at(dx, dy), device_id_type=MESH)
    loads = [
        pltpu.make_async_copy(source, target, w_recv.at[index])
        for index, (source, target) in enumerate(zip(weights_hbm, weights))
    ]
    for load in loads:
        load.start()

    def start_fields(s, i, j):
        for dx, dy in ((1, 1), (1, 0), (0, 1), (0, 0)):
            n = s * 4 + lax.rem(x + dx, 2) * 2 + lax.rem(y + dy, 2)
            a, b = i ^ dx, j ^ dy
            source = fields.at[n, pl.ds(a * half, half), b]
            target = fbuf.at[s, i * 2 + j, (1 - a) * 2 + (1 - b)]
            arrived = f_recv.at[s, i * 2 + j]
            if (dx, dy) == (0, 0):
                pltpu.make_async_copy(source, target, arrived).start()
            else:
                pltpu.make_async_remote_copy(
                    source, target, f_send, arrived,
                    device_id=at(dx * (2 * a - 1), dy * (2 * b - 1)), device_id_type=MESH,
                ).start()

    pl.semaphore_wait(barrier, len(reach))
    for s in range(sets):
        for i in range(2):
            for j in range(2):
                start_fields(s, i, j)

    for load in loads[:8]:
        load.wait()
    for index in range(3):
        wsplit[index] = mixer_fine[:, index * channels : (index + 1) * channels]
    row = lax.broadcasted_iota(jnp.int32, (tokens, tokens), 0)
    col = lax.broadcasted_iota(jnp.int32, (tokens, tokens), 1)
    parity, rest = row // patch, row % patch
    quadrant, within = rest // piece, rest % piece
    origin = (
        quadrant * (half * half)
        + (2 * (within // quarter) + parity % 2) * half
        + 2 * (within % quarter)
        + parity // 2
    )
    perm_fine[...] = (origin == col).astype(F32).astype(BF16)
    def send_merged(s, i, j):
        n = s * 4 + me
        w = i * 2 + j
        for pa in range(2):
            for pb in range(2):
                ox, oy = i - 1 + pa, j - 1 + pb
                part = pa * 2 + pb
                source = mbuf.at[s, w, part]
                target = mhome.at[n, 3 - part]
                local = pltpu.make_async_copy(source, target, m_recv)
                remote = pltpu.make_async_remote_copy(
                    source, target, m_send, m_recv, device_id=at(ox, oy), device_id_type=MESH
                )
                if oy == 0:
                    pl.when(ox == 0)(local.start)
                    pl.when(ox != 0)(remote.start)
                else:
                    remote.start()

    def send_owner(s, i, j):
        w = i * 2 + j
        for pa in range(2):
            for pb in range(2):
                ox, oy = i - 1 + pa, j - 1 + pb
                part = pa * 2 + pb
                farx, fary = ox == 2 * px - 1, oy == 2 * py - 1
                home = lax.rem(px + ox + 2, 2) * 2 + lax.rem(py + oy + 2, 2)
                source = mbuf.at[s, w, part]
                target = cbuf.at[s, home * 4 + 3 - part]
                far = jnp.logical_or(farx, fary)

                def keep(source=source, target=target):
                    target[...] = source[...]

                remote = pltpu.make_async_remote_copy(
                    source, target, c_send, c_recv.at[s],
                    device_id=at(jnp.where(farx, outx, 0), jnp.where(fary, outy, 0)),
                    device_id_type=MESH,
                )
                pl.when(far)(remote.start)
                pl.when(jnp.logical_not(far))(keep)

    group = 2

    def fine(step, carry):
        s, i = step // 2, step % 2

        values = []
        for j in range(group):
            w = i * 2 + j
            pltpu.make_async_copy(fbuf.at[s, w], fbuf.at[s, w], f_recv.at[s, w]).wait()
            window = fbuf[s, w].astype(F32).reshape(tokens, channels).astype(BF16)
            values.append(dot(perm_fine[...], window))
        value = jnp.concatenate(values, axis=0)
        normed = normalize(value, gain_window[...][None])
        q, k, v = (dot(normed, wsplit[index]).astype(BF16) for index in range(3))
        parts = [
            attention(*(t[w * tokens : (w + 1) * tokens] for t in (q, k, v)))
            for w in range(group)
        ]
        context = [jnp.concatenate(c, axis=0) for c in zip(*parts)]
        attended = (value + project(context, output_fine)).astype(BF16).astype(F32)
        normed = normalize(attended, gain_hidden[...][None])
        hidden = gelu(dot(normed, expand[...])).astype(BF16)
        refined = (attended + dot_nt(hidden, contract[...])).astype(BF16).astype(F32)
        slabs = [
            jnp.concatenate(
                [refined[w * tokens + p * patch : w * tokens + (p + 1) * patch] for w in range(group)],
                axis=0,
            )
            for p in range(4)
        ]
        mean = sum(jnp.sum(s, -1, keepdims=True) for s in slabs) * (1.0 / (4 * channels))
        slabs = [s - mean for s in slabs]
        spread = sum(jnp.sum(s * s, -1, keepdims=True) for s in slabs) * (1.0 / (4 * channels))
        scale = lax.rsqrt(spread + EPSILON)
        merged = None
        for p, slab in enumerate(slabs):
            gain = gain_merge[...][None, p * channels : (p + 1) * channels]
            part = dot(
                (slab * scale * gain).astype(BF16), merge_weight[p * channels : (p + 1) * channels, :]
            )
            merged = part if merged is None else merged + part
        merged = merged.astype(BF16)
        for j in range(group):
            mbuf[s, i * 2 + j] = merged[j * patch : (j + 1) * patch].reshape(4, piece, wide)
            send_merged(s, i, j)
            send_owner(s, i, j)
        return carry

    lax.fori_loop(0, sets * 2, fine, 0)

    bx, by = x - px, y - py

    def result_copy(s, home):
        hx, hy = bx + home // 2, by + home % 2
        n = s * 4 + me
        local = pltpu.make_async_copy(obuf.at[s, home], coarse_out.at[n], o_recv)
        remote = pltpu.make_async_remote_copy(
            obuf.at[s, home], coarse_out.at[n], o_send, o_recv,
            device_id=(hx, hy), device_id_type=MESH,
        )
        return home == me, local, remote

    sides = (1 - px, px)

    def coarse(s, carry):
        pltpu.make_async_copy(cbuf.at[s, pl.ds(0, 7)], cbuf.at[s, pl.ds(0, 7)], c_recv.at[s]).wait()
        merged = jnp.concatenate(
            [cbuf[s, pl.ds(8 * part, 8)].reshape(2 * patch, wide) for part in sides], axis=0
        ).astype(F32)
        normed = normalize(merged, gain_coarse[...][None])
        q, k, v = (
            dot(normed, mixer_coarse[:, index * wide : (index + 1) * wide]).astype(BF16)
            for index in range(3)
        )
        for index, part in enumerate(sides):
            rows = slice(index * 2 * patch, (index + 1) * 2 * patch)
            out = merged[rows] + project(attention(q[rows], k, v), output_coarse)
            obuf[s, pl.ds(2 * part, 2)] = out.astype(BF16).reshape(2, patch, wide)
            for column in range(2):
                here, local, remote = result_copy(s, 2 * part + column)
                pl.when(here)(local.start)
                pl.when(jnp.logical_not(here))(remote.start)
        return carry

    for load in loads[8:]:
        load.wait()
    lax.fori_loop(0, sets, coarse, 0)

    pltpu.make_async_copy(mhome, mhome, m_recv).wait()

    for ref, sem in (
        (fbuf.at[:, :, pl.ds(0, 3)], f_send),
        (mhome.at[pl.ds(0, sets * 3)], m_send),
        (cbuf.at[:, pl.ds(0, 7)], c_send),
        (obuf.at[:, pl.ds(0, 3)], o_send),
    ):
        pltpu.make_async_copy(ref, ref, sem).wait()
    pltpu.make_async_copy(coarse_out, coarse_out, o_recv).wait()


def natural_order(half, merged, coarse, merged_out, coarse_out):
    quarter = half // 2
    piece = quarter * quarter
    patch = 4 * piece
    row = lax.broadcasted_iota(jnp.int32, (patch, patch), 0)
    col = lax.broadcasted_iota(jnp.int32, (patch, patch), 1)
    down, across = row // half, row % half
    origin = (
        (down // quarter * 2 + across // quarter) * piece
        + (down % quarter) * quarter
        + across % quarter
    )
    order = (origin == col).astype(F32).astype(BF16)
    for n in range(merged.shape[0]):
        merged_out[n] = dot(order, merged[n]).astype(BF16)
        coarse_out[n] = dot(order, coarse[n]).astype(BF16)


def shards(nx, ny, fields, *weights):
    samples, side, _, channels = fields.shape
    half = side // 2
    sets = samples // 4
    wide = weights[7].shape[-1]
    piece = half * half // 4
    weights = [*weights[:5], weights[5].T, *weights[6:]]
    pieces = jax.ShapeDtypeStruct((samples, 4, piece, wide), BF16)
    shape = jax.ShapeDtypeStruct((samples, 4 * piece, wide), BF16)
    hbm = pl.BlockSpec(memory_space=pl.ANY)
    dma = pltpu.SemaphoreType.DMA
    merged, coarse = pl.pallas_call(
        functools.partial(kernel, nx, ny),
        out_shape=(pieces, shape),
        in_specs=[hbm] * (1 + len(weights)),
        out_specs=(hbm, hbm),
        scratch_shapes=[pltpu.VMEM(w.shape, w.dtype) for w in weights] + [
            pltpu.VMEM((sets, 4, 4, half, half, channels), BF16),
            pltpu.VMEM((sets, 4, 4, piece, wide), BF16),
            pltpu.VMEM((sets, 16, piece, wide), BF16),
            pltpu.VMEM((sets, 4, 4 * piece, wide), BF16),
            pltpu.VMEM((3, channels, channels), BF16),
            pltpu.VMEM((side * side, side * side), BF16),
            dma, dma((sets, 4)),
            dma, dma,
            dma, dma((sets,)),
            dma, dma,
            dma((len(weights),)),
        ],
        compiler_params=pltpu.CompilerParams(
            collective_id=0, has_side_effects=True, vmem_limit_bytes=62 * 1024 * 1024
        ),
        name="encoder",
    )(fields.reshape(samples, side, 2, half, channels), *weights)
    steps = 2
    block = pl.BlockSpec((samples // steps, 4 * piece, wide), lambda step: (step, 0, 0))
    merged, coarse = pl.pallas_call(
        functools.partial(natural_order, half),
        grid=(steps,),
        out_shape=(shape, shape),
        in_specs=[block] * 2,
        out_specs=(block, block),
        name="natural_order",
    )(merged.reshape(shape.shape), coarse)
    return tuple(t.reshape(samples, half, half, wide) for t in (merged, coarse))


def solution(mesh):
    in_specs = (P(None, "gx", "gy", None),) + (P(),) * 11
    out_specs = (P(None, "gx", "gy", None), P(None, "gx", "gy", None))
    body = functools.partial(shards, mesh.shape["gx"], mesh.shape["gy"])
    return jax.shard_map(body, mesh=mesh, in_specs=in_specs, out_specs=out_specs, check_vma=False)
```

```python
import functools
import math

import jax
import jax.numpy as jnp
from jax import lax
from jax.experimental import pallas as pl
from jax.experimental.pallas import tpu as pltpu
from jax.sharding import PartitionSpec as P

HEAD = 32
LANES = 128
EPSILON = 1e-05
F32 = jnp.float32
BF16 = jnp.bfloat16
MESH = pl.DeviceIdType.MESH


def dot(a, b):
    return jnp.dot(a, b, preferred_element_type=F32)


def dot_nt(a, b):
    return lax.dot_general(a, b, (((1,), (1,)), ((), ())), preferred_element_type=F32)


def normalize(values, gain):
    center = values - jnp.mean(values, -1, keepdims=True)
    spread = jnp.mean(center * center, -1, keepdims=True)
    return (center * lax.rsqrt(spread + EPSILON) * gain).astype(BF16)


def dot_tn(a, b):
    return lax.dot_general(a, b, (((0,), (0,)), ((), ())), preferred_element_type=F32)


def attention(queries, keys, values):
    channels, tokens = queries[0].shape
    ones = jnp.ones((16, tokens), BF16)
    units = [(w, row) for row in range(0, channels, HEAD) for w in range(len(queries))]

    def score(w, row):
        low = row // LANES * LANES
        width = min(LANES, channels - low)
        first = row - low
        parts = [queries[w][row : row + HEAD]]
        if first > 0:
            parts.insert(0, jnp.zeros((first, tokens), BF16))
        if width > first + HEAD:
            parts.append(jnp.zeros((width - first - HEAD, tokens), BF16))
        return dot(keys[w][:, low : low + width], jnp.concatenate(parts, axis=0))

    def weigh(w, row, powers):
        part = dot(jnp.concatenate([values[w][row : row + HEAD], ones], axis=0), powers)
        return part[:HEAD] * (1.0 / part[HEAD : HEAD + 1])

    depth = 6
    scores, highest, found = {}, {}, [[] for _ in queries]
    for step in range(len(units) + depth):
        if step < len(units):
            scores[step] = score(*units[step])
            highest[step] = jnp.max(scores[step], 0, keepdims=True)
        done = step - depth
        if done >= 0:
            powers = jnp.exp2(scores.pop(done) - highest.pop(done)).astype(BF16)
            found[units[done][0]].append(weigh(*units[done], powers))
    return [jnp.concatenate(f, axis=0).astype(BF16) for f in found]


def kernel(
    nx, ny,
    fields, *refs
):
    count = (len(refs) - 18) // 2
    weights_hbm, (mhome, coarse_out) = refs[:count], refs[count : count + 2]
    weights = refs[count + 2 : 2 * count + 2]
    (
        gain_window, mixer_fine, output_fine, gain_hidden, expand, contract,
        gain_merge, merge_weight, gain_coarse, mixer_coarse, output_coarse,
    ) = weights
    (
    fbuf, mbuf, cbuf, obuf, wsplit, wcoarse, perm_fine,
    f_send, f_recv, m_send, m_recv, c_send, c_recv, o_send, o_recv,
    w_recv,
    ) = refs[2 * count + 2 :]
    sets, _, _, half, _, channels = fbuf.shape
    side = 2 * half
    tokens = side * side
    quarter = half // 2
    piece = quarter * quarter
    patch = 4 * piece
    wide = mhome.shape[-1]
    x = lax.axis_index("gx")
    y = lax.axis_index("gy")
    px, py = x % 2, y % 2
    me = px * 2 + py

    def at(dx, dy):
        return (lax.rem(x + dx + nx, nx), lax.rem(y + dy + ny, ny))

    outx, outy = 2 * (2 * px - 1), 2 * (2 * py - 1)
    reach = [(dx, dy) for dx in (-1, 0, 1) for dy in (-1, 0, 1) if (dx, dy) != (0, 0)]
    for sign in (-1, 1):
        reach += [(sign * outx, 0), (0, sign * outy), (sign * outx, sign * outy)]
    barrier = pltpu.get_barrier_semaphore()
    for dx, dy in reach:
        pl.semaphore_signal(barrier, inc=1, device_id=at(dx, dy), device_id_type=MESH)
    loads = [
        pltpu.make_async_copy(source, target, w_recv.at[index])
        for index, (source, target) in enumerate(zip(weights_hbm, weights))
    ]
    for load in loads:
        load.start()

    def start_fields(s, i, j):
        for dx, dy in ((1, 1), (1, 0), (0, 1), (0, 0)):
            n = s * 4 + lax.rem(x + dx, 2) * 2 + lax.rem(y + dy, 2)
            a, b = lax.rem(i + dx, 2), j ^ dy
            source = fields.at[n, pl.ds(a * half, half), b]
            target = fbuf.at[s, i * 2 + j, (1 - a) * 2 + (1 - b)]
            arrived = f_recv.at[s, i * 2 + j]
            if (dx, dy) == (0, 0):
                pltpu.make_async_copy(source, target, arrived).start()
            else:
                pltpu.make_async_remote_copy(
                    source, target, f_send, arrived,
                    device_id=at(dx * (2 * a - 1), dy * (2 * b - 1)), device_id_type=MESH,
                ).start()

    pl.semaphore_wait(barrier, len(reach))
    def start_step(step):
        for j in range(2):
            start_fields(step // 2, step % 2, j)

    steps = 2 * sets
    ahead = min(2, steps)
    for step in range(ahead):
        start_step(step)

    for load in loads[:8]:
        load.wait()
    for index in range(3):
        part = mixer_fine[:, index * channels : (index + 1) * channels]
        wsplit[index] = part if index == 1 else part.T
    row = lax.broadcasted_iota(jnp.int32, (tokens, tokens), 0)
    col = lax.broadcasted_iota(jnp.int32, (tokens, tokens), 1)
    parity, rest = row // patch, row % patch
    quadrant, within = rest // piece, rest % piece
    origin = (
        quadrant * (half * half)
        + (2 * (within // quarter) + parity % 2) * half
        + 2 * (within % quarter)
        + parity // 2
    )
    perm_fine[...] = (origin == col).astype(F32).astype(BF16)
    def send_merged(s, i, j):
        n = s * 4 + me
        w = i * 2 + j
        for pa in range(2):
            for pb in range(2):
                ox, oy = i - 1 + pa, j - 1 + pb
                part = pa * 2 + pb
                source = mbuf.at[s, w, part]
                target = mhome.at[n, 3 - part]
                local = pltpu.make_async_copy(source, target, m_recv)
                remote = pltpu.make_async_remote_copy(
                    source, target, m_send, m_recv, device_id=at(ox, oy), device_id_type=MESH
                )
                if oy == 0:
                    pl.when(ox == 0)(local.start)
                    pl.when(ox != 0)(remote.start)
                else:
                    remote.start()

    def send_owner(s, i, j):
        w = i * 2 + j
        for pa in range(2):
            for pb in range(2):
                ox, oy = i - 1 + pa, j - 1 + pb
                part = pa * 2 + pb
                farx, fary = ox == 2 * px - 1, oy == 2 * py - 1
                home = lax.rem(px + ox + 2, 2) * 2 + lax.rem(py + oy + 2, 2)
                source = mbuf.at[s, w, part]
                target = cbuf.at[s, home * 4 + 3 - part]
                far = jnp.logical_or(farx, fary)

                def keep(source=source, target=target):
                    target[...] = source[...]

                remote = pltpu.make_async_remote_copy(
                    source, target, c_send, c_recv.at[s],
                    device_id=at(jnp.where(farx, outx, 0), jnp.where(fary, outy, 0)),
                    device_id_type=MESH,
                )
                pl.when(far)(remote.start)
                pl.when(jnp.logical_not(far))(keep)

    group = 2
    factor = math.log2(math.e) / math.sqrt(HEAD)

    def fine(step, carry):
        s, i = step // 2, step % 2
        for j in range(group):
            w = i * 2 + j
            pltpu.make_async_copy(fbuf.at[s, w], fbuf.at[s, w], f_recv.at[s, w]).wait()

        @pl.when(step + ahead < steps)
        def _():
            start_step(step + ahead)

        windows = []
        for j in range(group):
            w = i * 2 + j
            window = fbuf[s, w].astype(F32).reshape(tokens, channels).astype(BF16)
            windows.append(dot(perm_fine[...], window))
        value = jnp.concatenate(windows, axis=0)
        normed = normalize(value, gain_window[...][None])
        queries = (dot_nt(wsplit[0], normed) * factor).astype(BF16)
        keys = dot(normed, wsplit[1]).astype(BF16)
        values_t = dot_nt(wsplit[2], normed).astype(BF16)
        spans = [slice(w * tokens, (w + 1) * tokens) for w in range(group)]
        context = jnp.concatenate(
            attention(
                [queries[:, span] for span in spans],
                [keys[span] for span in spans],
                [values_t[:, span] for span in spans],
            ),
            axis=1,
        )
        attended = (value + dot_tn(context, output_fine[...])).astype(BF16).astype(F32)
        normed = normalize(attended, gain_hidden[...][None] * math.sqrt(0.5))
        hidden = dot(normed, expand[...])
        hidden = (hidden + hidden * lax.erf(hidden)).astype(BF16)
        refined = attended + dot_nt(hidden, contract[...]) * math.sqrt(0.5)
        refined = refined.astype(BF16).astype(F32)
        slabs = [
            jnp.concatenate(
                [refined[w * tokens + p * patch : w * tokens + (p + 1) * patch] for w in range(group)],
                axis=0,
            )
            for p in range(4)
        ]
        mean = sum(jnp.sum(s, -1, keepdims=True) for s in slabs) * (1.0 / (4 * channels))
        slabs = [s - mean for s in slabs]
        spread = sum(jnp.sum(s * s, -1, keepdims=True) for s in slabs) * (1.0 / (4 * channels))
        scale = lax.rsqrt(spread + EPSILON)
        merged = None
        for p, slab in enumerate(slabs):
            gain = gain_merge[...][None, p * channels : (p + 1) * channels]
            part = dot(
                (slab * scale * gain).astype(BF16), merge_weight[p * channels : (p + 1) * channels, :]
            )
            merged = part if merged is None else merged + part
        merged = merged.astype(BF16)
        for j in range(group):
            mbuf[s, i * 2 + j] = merged[j * patch : (j + 1) * patch].reshape(4, piece, wide)
            send_merged(s, i, j)
            send_owner(s, i, j)
        return carry

    lax.fori_loop(0, steps, fine, 0)

    bx, by = x - px, y - py

    def result_copy(s, home):
        hx, hy = bx + home // 2, by + home % 2
        n = s * 4 + me
        local = pltpu.make_async_copy(obuf.at[s, home], coarse_out.at[n], o_recv)
        remote = pltpu.make_async_remote_copy(
            obuf.at[s, home], coarse_out.at[n], o_send, o_recv,
            device_id=(hx, hy), device_id_type=MESH,
        )
        return home == me, local, remote

    sides = (1 - px, px)

    def coarse(s, carry):
        pltpu.make_async_copy(cbuf.at[s, pl.ds(0, 7)], cbuf.at[s, pl.ds(0, 7)], c_recv.at[s]).wait()
        merged = jnp.concatenate(
            [cbuf[s, pl.ds(8 * part, 8)].reshape(2 * patch, wide) for part in sides], axis=0
        ).astype(F32)
        normed = normalize(merged, gain_coarse[...][None])
        queries = (dot_nt(wcoarse[0], normed) * factor).astype(BF16)
        keys = dot(normed, mixer_coarse[:, wide : 2 * wide]).astype(BF16)
        values = dot_nt(wcoarse[1], normed).astype(BF16)
        result = merged + dot_tn(attention([queries], [keys], [values])[0], output_coarse[...])
        for index, part in enumerate(sides):
            rows = slice(index * 2 * patch, (index + 1) * 2 * patch)
            obuf[s, pl.ds(2 * part, 2)] = result[rows].astype(BF16).reshape(2, patch, wide)
            for column in range(2):
                here, local, remote = result_copy(s, 2 * part + column)
                pl.when(here)(local.start)
                pl.when(jnp.logical_not(here))(remote.start)
        return carry

    for load in loads[8:]:
        load.wait()
    wcoarse[0] = mixer_coarse[:, :wide].T
    wcoarse[1] = mixer_coarse[:, 2 * wide :].T
    lax.fori_loop(0, sets, coarse, 0)

    pltpu.make_async_copy(mhome, mhome, m_recv).wait()

    for ref, sem in (
        (fbuf.at[:, :, pl.ds(0, 3)], f_send),
        (mhome.at[pl.ds(0, sets * 3)], m_send),
        (cbuf.at[:, pl.ds(0, 7)], c_send),
        (obuf.at[:, pl.ds(0, 3)], o_send),
    ):
        pltpu.make_async_copy(ref, ref, sem).wait()
    pltpu.make_async_copy(coarse_out, coarse_out, o_recv).wait()


def natural_order(half, merged, coarse, merged_out, coarse_out):
    quarter = half // 2
    piece = quarter * quarter
    patch = 4 * piece
    row = lax.broadcasted_iota(jnp.int32, (patch, patch), 0)
    col = lax.broadcasted_iota(jnp.int32, (patch, patch), 1)
    down, across = row // half, row % half
    origin = (
        (down // quarter * 2 + across // quarter) * piece
        + (down % quarter) * quarter
        + across % quarter
    )
    order = (origin == col).astype(F32).astype(BF16)
    for n in range(merged.shape[0]):
        merged_out[n] = dot(order, merged[n]).astype(BF16)
        coarse_out[n] = dot(order, coarse[n]).astype(BF16)


def shards(nx, ny, fields, *weights):
    samples, side, _, channels = fields.shape
    half = side // 2
    sets = samples // 4
    wide = weights[7].shape[-1]
    piece = half * half // 4
    weights = [*weights[:5], weights[5].T, *weights[6:]]
    pieces = jax.ShapeDtypeStruct((samples, 4, piece, wide), BF16)
    shape = jax.ShapeDtypeStruct((samples, 4 * piece, wide), BF16)
    hbm = pl.BlockSpec(memory_space=pl.ANY)
    dma = pltpu.SemaphoreType.DMA
    merged, coarse = pl.pallas_call(
        functools.partial(kernel, nx, ny),
        out_shape=(pieces, shape),
        in_specs=[hbm] * (1 + len(weights)),
        out_specs=(hbm, hbm),
        scratch_shapes=[pltpu.VMEM(w.shape, w.dtype) for w in weights] + [
            pltpu.VMEM((sets, 4, 4, half, half, channels), BF16),
            pltpu.VMEM((sets, 4, 4, piece, wide), BF16),
            pltpu.VMEM((sets, 16, piece, wide), BF16),
            pltpu.VMEM((sets, 4, 4 * piece, wide), BF16),
            pltpu.VMEM((3, channels, channels), BF16),
            pltpu.VMEM((2, wide, wide), BF16),
            pltpu.VMEM((side * side, side * side), BF16),
            dma, dma((sets, 4)),
            dma, dma,
            dma, dma((sets,)),
            dma, dma,
            dma((len(weights),)),
        ],
        compiler_params=pltpu.CompilerParams(
            collective_id=0, has_side_effects=True, vmem_limit_bytes=62 * 1024 * 1024
        ),
        name="encoder",
    )(fields.reshape(samples, side, 2, half, channels), *weights)
    steps = 2
    block = pl.BlockSpec((samples // steps, 4 * piece, wide), lambda step: (step, 0, 0))
    merged, coarse = pl.pallas_call(
        functools.partial(natural_order, half),
        grid=(steps,),
        out_shape=(shape, shape),
        in_specs=[block] * 2,
        out_specs=(block, block),
        name="natural_order",
    )(merged.reshape(shape.shape), coarse)
    return tuple(t.reshape(samples, half, half, wide) for t in (merged, coarse))


def solution(mesh):
    in_specs = (P(None, "gx", "gy", None),) + (P(),) * 11
    out_specs = (P(None, "gx", "gy", None), P(None, "gx", "gy", None))
    body = functools.partial(shards, mesh.shape["gx"], mesh.shape["gy"])
    return jax.shard_map(body, mesh=mesh, in_specs=in_specs, out_specs=out_specs, check_vma=False)
```

```python
import functools
import math

import jax
import jax.numpy as jnp
from jax import lax
from jax.experimental import pallas as pl
from jax.experimental.pallas import tpu as pltpu
from jax.sharding import PartitionSpec as P

HEAD = 32
LANES = 128
EPSILON = 1e-05
F32 = jnp.float32
BF16 = jnp.bfloat16
MESH = pl.DeviceIdType.MESH


def dot(a, b):
    return jnp.dot(a, b, preferred_element_type=F32)


def dot_nt(a, b):
    return lax.dot_general(a, b, (((1,), (1,)), ((), ())), preferred_element_type=F32)


def normalize(values, gain):
    center = values - jnp.mean(values, -1, keepdims=True)
    spread = jnp.mean(center * center, -1, keepdims=True)
    return (center * lax.rsqrt(spread + EPSILON) * gain).astype(BF16)


def dot_tn(a, b):
    return lax.dot_general(a, b, (((0,), (0,)), ((), ())), preferred_element_type=F32)


def attention(queries, keys, values, filler=iter(())):
    channels, tokens = queries[0].shape
    ones = jnp.ones((16, values[0].shape[1]), BF16)
    units = [(w, row) for row in range(0, channels, HEAD) for w in range(len(queries))]

    def score(w, row):
        low = row // LANES * LANES
        width = min(LANES, channels - low)
        first = row - low
        parts = [queries[w][row : row + HEAD]]
        if first > 0:
            parts.insert(0, jnp.zeros((first, tokens), BF16))
        if width > first + HEAD:
            parts.append(jnp.zeros((width - first - HEAD, tokens), BF16))
        return dot(keys[w][:, low : low + width], jnp.concatenate(parts, axis=0))

    def weigh(w, row, powers):
        part = dot(jnp.concatenate([values[w][row : row + HEAD], ones], axis=0), powers)
        return part[:HEAD] * (1.0 / part[HEAD : HEAD + 1])

    depth = 6
    scores, highest, found = {}, {}, [[] for _ in queries]
    for step in range(len(units) + depth):
        if step < len(units):
            scores[step] = score(*units[step])
            highest[step] = jnp.max(scores[step], 0, keepdims=True)
        done = step - depth
        if done >= 0:
            powers = jnp.exp2((scores.pop(done) - highest.pop(done)).astype(BF16))
            found[units[done][0]].append(weigh(*units[done], powers))
        next(filler, None)
    return [jnp.concatenate(f, axis=0).astype(BF16) for f in found]


def kernel(
    nx, ny,
    fields, *refs
):
    count = (len(refs) - 23) // 2
    weights_hbm, (mhome, coarse_out) = refs[:count], refs[count : count + 2]
    weights = refs[count + 2 : 2 * count + 2]
    (
        gain_window, mixer_fine, output_fine, gain_hidden, expand, contract,
        gain_merge, merge_weight, gain_coarse, mixer_coarse, output_coarse,
    ) = weights
    (
    staged, packed, fbuf, mbuf, cbuf, obuf, wsplit, wcoarse, perm_fine, held_value, held_context,
    f_send, f_recv, m_send, m_recv, c_send, c_recv, o_send, o_recv,
    w_recv, h_recv,
    ) = refs[2 * count + 2 :]
    _, _, _, half, channels = staged.shape
    sets = fbuf.shape[0]
    side = 2 * half
    tokens = side * side
    quarter = half // 2
    piece = quarter * quarter
    patch = 4 * piece
    wide = mhome.shape[-1]
    x = lax.axis_index("gx")
    y = lax.axis_index("gy")
    px, py = x % 2, y % 2
    me = px * 2 + py

    def at(dx, dy):
        return (lax.rem(x + dx + nx, nx), lax.rem(y + dy + ny, ny))

    whole = pltpu.make_async_copy(fields, staged, h_recv)
    whole.start()
    ORDER = ((0, 0), (0, 1), (1, 0), (1, 1))
    outx, outy = 2 * (2 * px - 1), 2 * (2 * py - 1)
    reach = [(dx, dy) for dx in (-1, 0, 1) for dy in (-1, 0, 1) if (dx, dy) != (0, 0)]
    for sign in (-1, 1):
        reach += [(sign * outx, 0), (0, sign * outy), (sign * outx, sign * outy)]
    barrier = pltpu.get_barrier_semaphore()
    for dx, dy in reach:
        pl.semaphore_signal(barrier, inc=1, device_id=at(dx, dy), device_id_type=MESH)
    loads = [
        pltpu.make_async_copy(source, target, w_recv.at[index])
        for index, (source, target) in enumerate(zip(weights_hbm, weights))
    ]
    for load in loads:
        load.start()

    cells = half * half
    low_cells = cells // 2

    def pack(s, carry):
        for dx, dy in ORDER:
            n = s * 4 + lax.rem(x + dx, 2) * 2 + lax.rem(y + dy, 2)
            for a, b in ORDER:
                block = staged[n, a * half : (a + 1) * half, b].astype(F32).reshape(cells, channels)
                rest = block[:, LANES:]
                rest = jnp.concatenate([rest[:low_cells], rest[low_cells:]], axis=1)
                block = jnp.concatenate([block[:, :LANES], rest], axis=0).astype(BF16)
                if (dx, dy) == (0, 0):
                    fbuf[s, a * 2 + b, 3 - (a * 2 + b)] = block
                else:
                    packed[n, a * 2 + b] = block
        return carry

    whole.wait()
    lax.fori_loop(0, sets, pack, 0)

    def start_fields(s, i, j):
        for dx, dy in ((1, 1), (1, 0), (0, 1)):
            n = s * 4 + lax.rem(x + dx, 2) * 2 + lax.rem(y + dy, 2)
            a, b = lax.rem(i + dx, 2), j ^ dy
            pltpu.make_async_remote_copy(
                packed.at[n, a * 2 + b], fbuf.at[s, i * 2 + j, 3 - (a * 2 + b)],
                f_send.at[s * 2 + i], f_recv.at[s, i * 2 + j],
                device_id=at(dx * (2 * a - 1), dy * (2 * b - 1)), device_id_type=MESH,
            ).start()

    def start_step(step):
        for j in range(2):
            start_fields(step // 2, step % 2, j)

    steps = 2 * sets
    ahead = min(2, steps)
    pl.semaphore_wait(barrier, len(reach))
    start_step(0)

    def left(step):
        sent = fbuf.at[0, pl.ds(0, 2), pl.ds(0, 3)]
        pltpu.make_async_copy(sent, sent, f_send.at[step]).wait()

    for load in loads[:8]:
        load.wait()
    for index in range(3):
        part = mixer_fine[:, index * channels : (index + 1) * channels]
        wsplit[index] = part if index == 1 else part.T
    row = lax.broadcasted_iota(jnp.int32, (tokens, tokens), 0)
    col = lax.broadcasted_iota(jnp.int32, (tokens, tokens), 1)
    col = (
        col % (tokens // 2) // low_cells * cells
        + col // (tokens // 2) * low_cells
        + col % low_cells
    )
    parity, rest = row // patch, row % patch
    quadrant, within = rest // piece, rest % piece
    origin = (
        quadrant * (half * half)
        + (2 * (within // quarter) + parity % 2) * half
        + 2 * (within % quarter)
        + parity // 2
    )
    perm_fine[...] = (origin == col).astype(F32).astype(BF16)
    def send_merged(s, i, j):
        n = s * 4 + me
        w = i * 2 + j
        for pa in range(2):
            for pb in range(2):
                ox, oy = i - 1 + pa, j - 1 + pb
                part = pa * 2 + pb
                source = mbuf.at[s, w, part]
                target = mhome.at[n, 3 - part]
                local = pltpu.make_async_copy(source, target, m_recv)
                remote = pltpu.make_async_remote_copy(
                    source, target, m_send, m_recv, device_id=at(ox, oy), device_id_type=MESH
                )
                if oy == 0:
                    pl.when(ox == 0)(local.start)
                    pl.when(ox != 0)(remote.start)
                else:
                    remote.start()

    def send_owner(s, i, j):
        w = i * 2 + j
        for pa in range(2):
            for pb in range(2):
                ox, oy = i - 1 + pa, j - 1 + pb
                part = pa * 2 + pb
                farx, fary = ox == 2 * px - 1, oy == 2 * py - 1
                home = lax.rem(px + ox + 2, 2) * 2 + lax.rem(py + oy + 2, 2)
                source = mbuf.at[s, w, part]
                target = cbuf.at[s, home * 4 + 3 - part]
                far = jnp.logical_or(farx, fary)

                def keep(source=source, target=target):
                    target[...] = source[...]

                remote = pltpu.make_async_remote_copy(
                    source, target, c_send, c_recv.at[s],
                    device_id=at(jnp.where(farx, outx, 0), jnp.where(fary, outy, 0)),
                    device_id_type=MESH,
                )
                pl.when(far)(remote.start)
                pl.when(jnp.logical_not(far))(keep)

    group = 2
    factor = math.log2(math.e) / math.sqrt(HEAD)

    def front(step, filler):
        s, i = step // 2, step % 2
        for j in range(group):
            w = i * 2 + j
            three = fbuf.at[s, w, pl.ds(0, 3)]
            pltpu.make_async_copy(three, three, f_recv.at[s, w]).wait()

        @pl.when(step + ahead < steps)
        def _():
            start_step(step + ahead)

        windows = []
        for j in range(group):
            w = i * 2 + j
            blocks = [fbuf[s, w, part] for part in range(4)]
            rest = jnp.concatenate([block[cells:] for block in blocks], axis=0)
            turned = pltpu.roll(rest.astype(F32), LANES // 2, 1).astype(BF16)
            window = jnp.concatenate(
                [
                    jnp.concatenate(
                        [block[:low_cells] for block in blocks]
                        + [block[low_cells:cells] for block in blocks],
                        axis=0,
                    ),
                    jnp.concatenate([rest, turned], axis=0),
                ],
                axis=1,
            )
            windows.append(dot(perm_fine[...], window)[:, :channels])
        value = jnp.concatenate(windows, axis=0)
        next(filler, None)
        normed = normalize(value, gain_window[...][None])
        queries = (dot_nt(wsplit[0], normed) * factor).astype(BF16)
        next(filler, None)
        keys = dot(normed, wsplit[1]).astype(BF16)
        next(filler, None)
        values_t = dot_nt(wsplit[2], normed).astype(BF16)
        spans = [slice(w * tokens, (w + 1) * tokens) for w in range(group)]
        context = jnp.concatenate(
            attention(
                [queries[:, span] for span in spans],
                [keys[span] for span in spans],
                [values_t[:, span] for span in spans],
                filler,
            ),
            axis=1,
        )
        for _ in filler:
            pass
        held_value[...] = value
        held_context[...] = context

    def back(step, pieces):
        size = group * tokens // pieces
        s, i = step // 2, step % 2
        refined = []
        for w in range(pieces):
            rows = slice(w * size, (w + 1) * size)
            update = dot_tn(held_context[:, rows], output_fine[...])
            attended = (held_value[rows] + update).astype(BF16).astype(F32)
            normed = normalize(attended, gain_hidden[...][None] * math.sqrt(0.5))
            yield
            hidden = []
            for low in range(0, expand.shape[1], 256):
                part = dot(normed, expand[:, low : low + 256])
                hidden.append((part + part * lax.erf(part)).astype(BF16))
                yield
            update = dot_nt(jnp.concatenate(hidden, axis=1), contract[...])
            refined.append((attended + update * math.sqrt(0.5)).astype(BF16).astype(F32))
            yield
        refined = jnp.concatenate(refined, axis=0)
        refined = [refined[w * tokens : (w + 1) * tokens] for w in range(group)]
        slabs = [
            jnp.concatenate([r[p * patch : (p + 1) * patch] for r in refined], axis=0)
            for p in range(4)
        ]
        mean = sum(jnp.sum(s, -1, keepdims=True) for s in slabs) * (1.0 / (4 * channels))
        slabs = [s - mean for s in slabs]
        yield
        spread = sum(jnp.sum(s * s, -1, keepdims=True) for s in slabs) * (1.0 / (4 * channels))
        scale = lax.rsqrt(spread + EPSILON)
        merged = None
        for p, slab in enumerate(slabs):
            gain = gain_merge[...][None, p * channels : (p + 1) * channels]
            part = dot(
                (slab * scale * gain).astype(BF16), merge_weight[p * channels : (p + 1) * channels, :]
            )
            merged = part if merged is None else merged + part
            yield
        merged = merged.astype(BF16)
        for j in range(group):
            mbuf[s, i * 2 + j] = merged[j * patch : (j + 1) * patch].reshape(4, piece, wide)

    def send(step):
        for j in range(group):
            send_merged(step // 2, step % 2, j)
            send_owner(step // 2, step % 2, j)

    def fine(step, carry):
        front(step, back(step - 1, 1))
        send(step - 1)
        return carry

    left(0)
    if steps > 1:
        start_step(1)
    front(0, iter(()))
    lax.fori_loop(1, steps, fine, 0)
    for _ in back(steps - 1, 1):
        pass
    send(steps - 1)

    bx, by = x - px, y - py

    def result_copy(s, home):
        hx, hy = bx + home // 2, by + home % 2
        n = s * 4 + me
        local = pltpu.make_async_copy(obuf.at[s, home], coarse_out.at[n], o_recv)
        remote = pltpu.make_async_remote_copy(
            obuf.at[s, home], coarse_out.at[n], o_send, o_recv,
            device_id=(hx, hy), device_id_type=MESH,
        )
        return home == me, local, remote

    sides = (1 - px, px)

    def coarse(split, s, carry):
        pltpu.make_async_copy(cbuf.at[s, pl.ds(0, 7)], cbuf.at[s, pl.ds(0, 7)], c_recv.at[s]).wait()
        merged = jnp.concatenate(
            [cbuf[s, pl.ds(8 * part, 8)].reshape(2 * patch, wide) for part in sides], axis=0
        ).astype(F32)
        normed = normalize(merged, gain_coarse[...][None])
        queries = (dot_nt(wcoarse[0], normed) * factor).astype(BF16)
        keys = dot(normed, mixer_coarse[:, wide : 2 * wide]).astype(BF16)
        values = dot_nt(wcoarse[1], normed).astype(BF16)
        if split:
            cuts = [slice(index * 2 * patch, (index + 1) * 2 * patch) for index in range(2)]
        else:
            cuts = [slice(0, 4 * patch)]
        for first, cut in enumerate(cuts):
            context = attention([queries[:, cut]], [keys], [values])[0]
            result = (merged[cut] + dot_tn(context, output_coarse[...])).astype(BF16)
            for index, part in enumerate(sides):
                if split and index != first:
                    continue
                start = 0 if split else index * 2 * patch
                obuf[s, pl.ds(2 * part, 2)] = result[start : start + 2 * patch].reshape(2, patch, wide)
                for column in range(2):
                    here, local, remote = result_copy(s, 2 * part + column)
                    if index == 0:
                        remote.start()
                    else:
                        pl.when(here)(local.start)
                        pl.when(jnp.logical_not(here))(remote.start)
        return carry

    for load in loads[8:]:
        load.wait()
    wcoarse[0] = mixer_coarse[:, :wide].T
    wcoarse[1] = mixer_coarse[:, 2 * wide :].T
    lax.fori_loop(0, sets - 1, functools.partial(coarse, False), 0)
    coarse(False, sets - 1, 0)

    pltpu.make_async_copy(mhome, mhome, m_recv).wait()

    for step in range(1, steps):
        left(step)
    for ref, sem in (
        (mhome.at[pl.ds(0, sets * 3)], m_send),
        (cbuf.at[:, pl.ds(0, 7)], c_send),
        (obuf.at[:, pl.ds(0, 3)], o_send),
    ):
        pltpu.make_async_copy(ref, ref, sem).wait()
    pltpu.make_async_copy(coarse_out, coarse_out, o_recv).wait()


def natural_order(half, merged, coarse, merged_out, coarse_out):
    quarter = half // 2
    piece = quarter * quarter
    for source, target in ((merged, merged_out), (coarse, coarse_out)):
        values = source[...].astype(F32)
        rows = []
        for down in range(half):
            start = down // quarter * 2 * piece + down % quarter * quarter
            rows += [values[:, at : at + quarter] for at in (start, start + piece)]
        target[...] = jnp.concatenate(rows, axis=1).astype(BF16)


def shards(nx, ny, fields, *weights):
    samples, side, _, channels = fields.shape
    half = side // 2
    sets = samples // 4
    wide = weights[7].shape[-1]
    piece = half * half // 4
    weights = [*weights[:5], weights[5].T, *weights[6:]]
    pieces = jax.ShapeDtypeStruct((samples, 4, piece, wide), BF16)
    shape = jax.ShapeDtypeStruct((samples, 4 * piece, wide), BF16)
    hbm = pl.BlockSpec(memory_space=pl.ANY)
    dma = pltpu.SemaphoreType.DMA
    merged, coarse = pl.pallas_call(
        functools.partial(kernel, nx, ny),
        out_shape=(pieces, shape),
        in_specs=[hbm] * (1 + len(weights)),
        out_specs=(hbm, hbm),
        scratch_shapes=[pltpu.VMEM(w.shape, w.dtype) for w in weights] + [
            pltpu.VMEM((samples, side, 2, half, channels), BF16),
            pltpu.VMEM((samples, 4, 3 * half * half // 2, LANES), BF16),
            pltpu.VMEM((sets, 4, 4, 3 * half * half // 2, LANES), BF16),
            pltpu.VMEM((sets, 4, 4, piece, wide), BF16),
            pltpu.VMEM((sets, 16, piece, wide), BF16),
            pltpu.VMEM((sets, 4, 4 * piece, wide), BF16),
            pltpu.VMEM((3, channels, channels), BF16),
            pltpu.VMEM((2, wide, wide), BF16),
            pltpu.VMEM((side * side, side * side), BF16),
            pltpu.VMEM((2 * side * side, channels), F32),
            pltpu.VMEM((channels, 2 * side * side), BF16),
            dma((2 * sets,)), dma((sets, 4)),
            dma, dma,
            dma, dma((sets,)),
            dma, dma,
            dma((len(weights),)), dma,
        ],
        compiler_params=pltpu.CompilerParams(
            collective_id=0, has_side_effects=True, vmem_limit_bytes=62 * 1024 * 1024
        ),
        name="encoder",
    )(fields.reshape(samples, side, 2, half, channels), *weights)
    steps = 2
    block = pl.BlockSpec((samples // steps, 4 * piece, wide), lambda step: (step, 0, 0))
    merged, coarse = pl.pallas_call(
        functools.partial(natural_order, half),
        grid=(steps,),
        out_shape=(shape, shape),
        in_specs=[block] * 2,
        out_specs=(block, block),
        name="natural_order",
    )(merged.reshape(shape.shape), coarse)
    return tuple(t.reshape(samples, half, half, wide) for t in (merged, coarse))


def solution(mesh):
    in_specs = (P(None, "gx", "gy", None),) + (P(),) * 11
    out_specs = (P(None, "gx", "gy", None), P(None, "gx", "gy", None))
    body = functools.partial(shards, mesh.shape["gx"], mesh.shape["gy"])
    return jax.shard_map(body, mesh=mesh, in_specs=in_specs, out_specs=out_specs, check_vma=False)
```
